128 devices in a mesh: grp: 4 (over y), dev: 32 (over z, x, core).
Axes of the slice: x: 4, y: 4, z: 4, core: 2. Of those that a mesh axis runs over, the one named last changes fastest.
Arguments:
- integral_slabs: bfloat16 [32, 512, 512], P('dev'), may hold values from -6 to 6
- slab_owner: int32 [32], replicated, may hold values from 0 to 31, each once
- pair_orbs: int32 [1024, 2], P(('grp', 'dev')), may hold values from 0 to 31, all different within a row; in each aligned block of 8 rows (0 to 7, 8 to 15, ...) at most 2 rows name the same one
- domain_bases: bfloat16 [1024, 512, 128], P(('grp', 'dev')), may hold values from -0.25 to 0.25
- amplitudes: bfloat16 [1024, 128, 128], P(('grp', 'dev')), may hold values from -6 to 6
- coupled: int32 [1024, 32], P(('grp', 'dev')), may hold values from 0 to 31
- coupled_len: int32 [1024], P(('grp', 'dev')), may hold values from 1 to 32, as said below
Outputs:
- residual: float32 [1024, 128, 128], P(('grp', 'dev'))
The draws below stay inside these ranges and needn't reach their ends.
Inputs may be any that keep to these rules, and one draw needn't show every extreme that they name: `slab_owner`: a permutation of the positions. `pair_orbs`: the two orbitals of a pair differ; among the pairs of one device no orbital is named more than 2 times. `coupled_len`: pair 0 uses all 32 slots.
All inputs are finite; a program needn't handle non-finite values.
Results may differ from the reference program's by a relative error of at most 0.005.
Values may be sent and summed in bfloat16 or wider, within the bound.
A program may use at most 128 MiB of HBM per device.

```python
import math
import jax
import jax.numpy as jnp
import numpy as np
from jax import lax

NAUX = 512
NORB = 512
NPNO = 128
P_DEV = 8
NCPL = 32
NOCC = 32
NPAIR = 1024
CAP = 2
N_GRP = 4
N_DEV = 32


def draw_coupled_len(key, part):
    listed = jax.random.randint(key, (NPAIR,), 1, NCPL + 1)
    return listed.at[0].set(NCPL).astype(jnp.int32)


def with_ends(drawn, key, low, high):
    longest = drawn.shape.index(max(drawn.shape))
    spots = []
    for shift in (0, 1):
        where = [jax.random.randint(jax.random.fold_in(key, axis), (), 0, length) for axis, length in enumerate(drawn.shape)]
        where[longest] = (where[longest] + shift) % drawn.shape[longest]
        spots.append(tuple(where))
    return drawn.at[spots[0]].set(low).at[spots[1]].set(high)


def shard_levels(rng, extent, cuts, least, high):
    def one(dim, blocks):
        draws = jax.random.uniform(jax.random.fold_in(jax.random.fold_in(rng, 6), dim), (blocks,), jnp.float32, least / len(cuts), high / len(cuts))
        return jnp.repeat(jnp.exp(draws), extent[dim] // blocks).reshape((-1,) + (1,) * (len(extent) - dim - 1))

    gain = one(*cuts[0])
    for cut in cuts[1:]:
        gain = gain * one(*cut)
    return gain


def shared_out(own_key, own, number, rows, count, top, bound, skew):
    ranking = jax.random.permutation(own_key, count)
    crowded, common = shares(count, rows * top, bound, skew, True), shares(count, rows * top, bound, skew, False)
    places = jnp.arange(count)

    def named(tallies, rotation):
        used = int((tallies > 0).sum())
        fixed = max(1, used // 4)
        shifted = fixed + (places - fixed + rotation * (used - fixed)) % max(1, count - fixed)
        return jnp.zeros((count,), jnp.int32).at[ranking[jnp.where(places < fixed, places, shifted)]].set(jnp.asarray(tallies, jnp.int32))

    tallies = jnp.where(number % 4 == 0, named(crowded, number // 4), named(common, number - number // 4 - 1))
    mixed = jax.random.permutation(jax.random.fold_in(own, 3), count)
    source_of, receiver = mixed[0:count // 2 * 2:2], mixed[1:count // 2 * 2:2]
    margin = jnp.minimum(tallies[source_of] - 1, bound - tallies[receiver]) // 2
    margin = jnp.where((source_of == ranking[0]) | (receiver == ranking[0]) | (tallies[receiver] == 0), 0, jnp.maximum(margin, 0))
    shifted = jax.random.randint(jax.random.fold_in(own, 4), (count // 2,), 0, 1 << 20) % (margin + 1)
    tallies = tallies.at[source_of].add(-shifted).at[receiver].add(shifted)
    labels = jnp.searchsorted(jnp.cumsum(tallies), jnp.arange(rows * top), side="right").astype(jnp.int32)
    listing = labels.reshape(top, rows).T
    listing = listing[jax.random.permutation(jax.random.fold_in(own, 1), rows)]
    rotation = jax.random.randint(jax.random.fold_in(own, 2), (rows, 1), 0, top)
    return jnp.take_along_axis(listing, (jnp.arange(top)[None, :] + rotation) % top, axis=1)


def shares(number_of, total, bound, skew, full):
    portions = [(1 << 20) // math.isqrt(standing ** skew) + 1 for standing in range(1, number_of + 1)]
    largest = bound if full else min(bound, max(-(-total // number_of), total * portions[0] // sum(portions)))
    least = 1 if total - largest >= number_of - 1 else 0
    holding, surplus = [largest] + [least] * (number_of - 1), total - largest - least * (number_of - 1)
    while surplus > 0:
        movable = [i for i in range(1, number_of) if holding[i] < largest] or [i for i in range(1, number_of) if holding[i] < bound]
        mass, left = sum([portions[i] for i in movable]), surplus
        for i in movable:
            more = min(bound - holding[i], max(1, left * portions[i] // mass), surplus)
            holding[i] = holding[i] + more
            surplus = surplus - more
    return np.array(holding)


def centred(stream_key, shape, spread, bound, shards=(), kind=jnp.bfloat16):
    values = spread * jax.random.normal(stream_key, shape, jnp.float32)
    if shards:
        values = values * shard_levels(stream_key, shape, shards, -0.22, 0.18)
    return jnp.clip(values, -bound, bound).astype(kind)


def setup_inputs(seed: int = 0) -> dict:
    keys = jax.random.split(jax.random.key(seed), 8)
    integral_slabs = centred(keys[0], (NOCC, NAUX, NORB), 1.0, 6.0, ((0, 32),))
    slab_owner = jax.random.permutation(keys[1], NOCC).astype(jnp.int32)
    pair_orbs_keys = jax.random.split(jax.random.fold_in(keys[2], 1), NPAIR // P_DEV)
    pair_orbs_turns = jax.random.permutation(jax.random.fold_in(keys[2], 3), NPAIR // P_DEV)
    pair_orbs = jax.vmap(lambda own, number: shared_out(jax.random.fold_in(keys[2], 2), own, number, P_DEV, NOCC, 2, CAP, 0))(pair_orbs_keys, pair_orbs_turns).reshape((NPAIR, 2))
    domain_bases = centred(keys[3], (NPAIR, NORB, NPNO), NORB ** -0.5, 0.25, ((0, 128),))
    amplitudes = centred(keys[4], (NPAIR, NPNO, NPNO), 1.0, 6.0, ((0, 128),))
    coupled = with_ends(jax.random.randint(keys[5], (NPAIR, NCPL), 0, N_GRP * P_DEV), jax.random.fold_in(keys[5], 1), 0, (N_GRP * P_DEV) - 1).astype(jnp.int32)
    coupled_len = draw_coupled_len(jax.random.fold_in(keys[7], 71), 0)
    return {"integral_slabs": integral_slabs, "slab_owner": slab_owner, "pair_orbs": pair_orbs, "domain_bases": domain_bases, "amplitudes": amplitudes, "coupled": coupled, "coupled_len": coupled_len}


def reference(integral_slabs, slab_owner, pair_orbs, domain_bases, amplitudes, coupled, coupled_len):
    pair_total = domain_bases.shape[0]
    pair_ids = jnp.arange(pair_total, dtype=jnp.int32)
    owner_device = pair_ids // P_DEV % N_DEV
    global_pairs = ((coupled // P_DEV * N_DEV + owner_device[:, None]) * P_DEV + coupled % P_DEV).astype(jnp.int32)
    inverse_root = 1.0 / math.sqrt(NAUX)

    def one_pair(pair_index):
        domain_basis = domain_bases[pair_index]
        first_slab = integral_slabs[slab_owner[pair_orbs[pair_index, 0]]]
        second_slab = integral_slabs[slab_owner[pair_orbs[pair_index, 1]]]
        half_left = jnp.dot(first_slab, domain_basis, preferred_element_type=jnp.float32).astype(jnp.bfloat16)
        half_right = jnp.dot(second_slab, domain_basis, preferred_element_type=jnp.float32).astype(jnp.bfloat16)
        exchange = jnp.dot(half_left.T, half_right, preferred_element_type=jnp.float32) * inverse_root
        chosen = global_pairs[pair_index]
        chosen_bases = domain_bases[chosen].astype(jnp.float32)
        chosen_amps = amplitudes[chosen].astype(jnp.float32)
        intersection = jnp.einsum('ra,krb->kab', domain_basis.astype(jnp.float32), chosen_bases).astype(jnp.bfloat16)
        projected = jnp.einsum('kab,kbc->kac', intersection.astype(jnp.float32), chosen_amps).astype(jnp.bfloat16)
        coupled_terms = jnp.einsum('kac,kdc->kad', projected.astype(jnp.float32), intersection.astype(jnp.float32))
        weights = (jnp.arange(NCPL) < coupled_len[pair_index]).astype(jnp.float32)
        coupled_sum = jnp.einsum('k,kad->ad', weights, coupled_terms)
        return exchange + NORB / NPNO * coupled_sum
    return lax.map(one_pair, pair_ids)
```

```python
import math

import jax
import jax.numpy as jnp
from jax import lax
from jax.experimental import pallas as pl
from jax.experimental.pallas import tpu as pltpu
from jax.sharding import PartitionSpec as P

NAUX, NORB, NPNO = 512, 512, 128
PDEV, NGRP = 8, 4
RING = 4
HALF = NAUX // 2
QUART = NAUX // 4
MESH = pl.DeviceIdType.MESH
BF16, F32 = jnp.bfloat16, jnp.float32
NT = (((1,), (1,)), ((), ()))
TN = (((0,), (0,)), ((), ()))


def mm(a, b, dims=None):
    if dims is None:
        return jnp.dot(a, b, preferred_element_type=F32)
    return lax.dot_general(a, b, dims, preferred_element_type=F32)


def kernel(
    slab_hbm, u_hbm, t_hbm, cpl_hbm, len_hbm, orb_hbm, owner_hbm, out_ref,
    ubuf, tbuf, meta, cpl, lenv, orbv, lens, orbs, owner, slabs, vbuf, bd, acc, rsend, rin,
    send_sem, y_sem, ym_sem, r_sem, net_sem, sib_sem, loc_sem,
):
    g = lax.axis_index("grp")
    d = lax.axis_index("dev")
    rem, div = lax.rem, lax.div
    c = rem(d, 2)
    x = rem(div(d, 2), RING)
    z = div(d, 2 * RING)
    up, dn = rem(g + 1, NGRP), rem(g + NGRP - 1, NGRP)
    half = rem(g, 2)
    sender2 = div(g, 2) == c
    heavy = div(up, 2) == c

    def dev(zz, xx, cc):
        return rem(zz, RING) * (2 * RING) + rem(xx, RING) * 2 + cc

    def seat(m, o, cc):
        zz = z + (m + (o - m) * c) + RING
        xx = x + (o + (m - o) * c) + RING
        return dev(zz, xx, cc)

    sib = dev(z, x, 1 - c)

    barrier = pltpu.get_barrier_semaphore()
    partners = [(up, d), (dn, d), (g, sib)]
    for dz, dx in ((1, 0), (-1, 0), (0, 1), (0, -1)):
        for cc in (0, 1):
            partners.append((g, dev(z + dz + RING, x + dx + RING, cc)))
    for pg, pd in partners:
        pl.semaphore_signal(barrier, inc=1, device_id=(pg, pd), device_id_type=MESH)


    def local(src, dst, i):
        cp = pltpu.make_async_copy(src, dst, loc_sem.at[i])
        cp.start()
        return cp

    lu = local(u_hbm, ubuf.at[0], 0)
    lt = local(t_hbm, tbuf.at[0], 1)
    lm = [local(cpl_hbm, cpl.at[0], 2), local(len_hbm, lens.at[0], 3)]
    lp = [local(orb_hbm, orbs.at[0], 5), local(owner_hbm, owner, 6)]
    my_rows = slab_hbm.at[pl.ds(half * HALF, HALF), :]
    ls = local(my_rows, slabs.at[d], 4)

    pl.semaphore_wait(barrier, len(partners))

    sent, sent_pred, sent_pred2 = [], [], []
    counter = [0]

    def make(refs, pg, pd):
        i = counter[0]
        counter[0] += 1

        def build():
            src, dst, recv = refs()
            return pltpu.make_async_remote_copy(
                src_ref=src, dst_ref=dst, send_sem=send_sem.at[i], recv_sem=recv,
                device_id=(pg, pd), device_id_type=MESH)
        return build

    def push(src, dst, recv, pg, pd):
        cp = make(lambda: (src, dst, recv), pg, pd)
        cp().start()
        sent.append(cp)

    def arrival(dst, recv):
        pltpu.make_async_remote_copy(
            src_ref=dst, dst_ref=dst, send_sem=send_sem.at[0], recv_sem=recv,
            device_id=(up, d), device_id_type=MESH).wait_recv()

    def y_step(k, row, pg):
        two = pl.ds(2 * k, 2)
        return [
            make(lambda: (u_hbm.at[two], ubuf.at[row, two], y_sem.at[row - 1, k, 0]), pg, d),
            make(lambda: (t_hbm.at[two], tbuf.at[row, two], y_sem.at[row - 1, k, 1]), pg, d),
        ]

    def start_y(k):
        for cp in y_step(k, 1, up):
            cp().start()
            sent.append(cp)

    def quarter(q):
        return slab_hbm.at[pl.ds(half * HALF + q * QUART, QUART), :]

    def slab_dst(s, q):
        return slabs.at[s, pl.ds(q * QUART, QUART), :]

    def y_meta(row, pg):
        return [
            make(lambda: (cpl_hbm, cpl.at[row], ym_sem.at[row - 1, 0]), pg, d),
            make(lambda: (len_hbm, lenv.at[row - 1], ym_sem.at[row - 1, 1]), pg, d),
        ]

    push(orb_hbm, orbv, ym_sem.at[0, 2], up, d)
    for cp in y_meta(1, up):
        cp().start()
        sent.append(cp)
    for k in range(1):
        start_y(k)
    for q, nbrs in ((0, ((0, 1), (0, -1))), (1, ((1, 0), (-1, 0))), (1, ((0, 1), (0, -1))), (0, ((1, 0), (-1, 0)))):
        for dz, dx in nbrs:
            push(quarter(q), slab_dst(d, q), net_sem.at[d], g, dev(z + dz + RING, x + dx + RING, q))
    push(my_rows, slabs.at[d], sib_sem.at[d], g, sib)
    for k in range(1, 4):
        start_y(k)

    @pl.when(sender2)
    def _():
        sent_pred.extend(y_meta(2, dn))
        for k in range(4):
            sent_pred.extend(y_step(k, 2, dn))
        for cp in sent_pred:
            cp().start()

    events = [(0, -1, 0), (0, 1, 1), (0, -1, 1), (0, 1, 0),
              (-1, 0, 0), (1, 0, 1), (-1, 0, 1), (1, 0, 0), (0, 2, 0), (0, 2, 1)]
    for o, k in ((-1, 0), (1, 1), (-1, 1), (1, 0)):
        events += [(-1, o, k), (1, o, k)]
    events += [(2, 0, 0), (2, 0, 1)]
    for o, k in ((2, 0), (2, 1)):
        events += [(-1, o, k), (1, o, k)]
    events += [(2, o, k) for o, k in ((-1, 0), (1, 1), (-1, 1), (1, 0), (2, 0), (2, 1))]
    all_pieces = list(events)

    def relay(n):
        for _ in range(min(n, len(events))):
            m, o, k = events.pop(0)
            s = seat(m, o, k)
            piece = slab_dst(s, c)
            arrival(piece, net_sem.at[s])
            if m == 0:
                if (o, k) == (-1, 0):
                    push(piece, piece, net_sem.at[s], g, seat(0, 1, c))
                if (o, k) == (1, 1):
                    push(piece, piece, net_sem.at[s], g, seat(0, -1, c))
                push(piece, piece, net_sem.at[s], g, seat(1, 0, c))
                push(piece, piece, net_sem.at[s], g, seat(-1, 0, c))
            elif (m, k) == (-1, 0):
                push(piece, piece, net_sem.at[s], g, seat(1, 0, c))
            elif (m, k) == (1, 1):
                push(piece, piece, net_sem.at[s], g, seat(-1, 0, c))
            push(piece, piece, sib_sem.at[s], g, sib)

    def transpose_pairs(row, j):
        for p in (2 * j, 2 * j + 1):
            vbuf[row, p * NPNO:(p + 1) * NPNO, :] = ubuf[row, p].T

    def build_bd(row, j):
        zero = jnp.zeros((NPNO, NPNO), BF16)
        top = jnp.concatenate([tbuf[row, 2 * j], zero], axis=1)
        bot = jnp.concatenate([zero, tbuf[row, 2 * j + 1]], axis=1)
        bd[row, j] = jnp.concatenate([top, bot], axis=0)

    def count(row, cand):
        hit = jnp.sum(jnp.where(meta[row] == cand, 4.0, 0.0), axis=1, keepdims=True)
        return jnp.broadcast_to(hit, (PDEV, NPNO))

    def group_of(row):
        return (g, dn, up)[row]

    def contrib(tgt, lo, n, src, j):
        uq = jnp.concatenate([ubuf[src, 2 * j], ubuf[src, 2 * j + 1]], axis=1)
        bdq = bd[src, j]
        cand = group_of(src) * PDEV + 2 * j
        w = jnp.concatenate([count(tgt, cand), count(tgt, cand + 1)], axis=1)
        for b in range(lo, lo + n, 2):
            rows = slice(b * NPNO, (b + 2) * NPNO)
            s = mm(vbuf[tgt, rows, :], uq).astype(BF16)
            proj = mm(s, bdq)
            for i in (0, 1):
                part = slice(i * NPNO, (i + 1) * NPNO)
                pw = (proj[part] * w[b + i:b + i + 1]).astype(BF16)
                at = slice((b + i) * NPNO, (b + i + 1) * NPNO)
                acc[tgt, at, :] += mm(pw, s[part], NT)

    def loop(n, fn):
        lax.fori_loop(0, n, lambda j, carry: (fn(j), carry)[1], 0)

    def exchange(row, lo, n):
        def one(t):
            i = owner[orbs[row, 0, t]]
            k = owner[orbs[row, 1, t]]
            u = ubuf[row, t]
            left = mm(slabs[i], u).astype(BF16)
            right = mm(slabs[k], u).astype(BF16)
            ex = mm(left, right, TN) * (1.0 / math.sqrt(NAUX))
            at = pl.ds(pl.multiple_of(t * NPNO, NPNO), NPNO)
            acc[row, at, :] += ex
        lax.fori_loop(lo, lo + n, lambda t, carry: (one(t), carry)[1], 0)

    def wait_y(row, k):
        two = pl.ds(2 * k, 2)
        arrival(ubuf.at[row, two], y_sem.at[row - 1, k, 0])
        arrival(tbuf.at[row, two], y_sem.at[row - 1, k, 1])

    def take_meta(row):
        rows = lax.broadcasted_iota(jnp.int32, (PDEV, 32), 0)
        used = jnp.zeros((PDEV, 32), jnp.int32)
        for p in range(PDEV):
            used = jnp.where(rows == p, lens[row, p], used)
        slot = lax.broadcasted_iota(jnp.int32, (PDEV, 32), 1)
        meta[row] = jnp.where(slot < used, cpl[row], -1)

    def arrive_meta(row):
        arrival(cpl.at[row], ym_sem.at[row - 1, 0])
        arrival(lenv.at[row - 1], ym_sem.at[row - 1, 1])
        cp = pltpu.make_async_copy(lenv.at[row - 1], lens.at[row], loc_sem.at[6 + row])
        cp.start()
        cp.wait()
        take_meta(row)

    acc[...] = jnp.zeros_like(acc)
    lu.wait()
    lt.wait()
    for j in range(4):
        transpose_pairs(0, j)
        build_bd(0, j)
    for cp in lm:
        cp.wait()
    take_meta(0)
    relay(4)
    loop(4, lambda j: contrib(0, 0, 8, 0, j))
    relay(6)
    arrive_meta(1)
    arrival(orbv, ym_sem.at[0, 2])
    lp1 = pltpu.make_async_copy(orbv, orbs.at[1], loc_sem.at[9])
    lp1.start()

    def tile1(k):
        wait_y(1, k)
        transpose_pairs(1, k)
        build_bd(1, k)
        contrib(0, 0, 8, 1, k)
        relay(2)
        loop(4, lambda j: contrib(1, 2 * k, 2, 0, j))
        relay(2)

    def tile2(k):
        loop(4, lambda j: contrib(1, 2 * k, 2, 2, j))

    def return1(k):
        two = pl.ds(2 * k, 2)
        rsend[0, 2 * k:2 * k + 2] = acc[1, 2 * k * NPNO:(2 * k + 2) * NPNO, :].astype(BF16).reshape(2, NPNO, NPNO)
        push(rsend.at[0, two], rin.at[0, two], r_sem.at[0, k], dn, d)

    def back2(b):
        two = pl.ds(2 * b, 2)
        return make(lambda: (rsend.at[1, two], rin.at[1, two], r_sem.at[1, b]), up, d)

    tile1(0)
    relay(4)
    tile1(1)
    relay(30)
    tile1(2)

    @pl.when(heavy)
    def _():
        arrive_meta(2)
        for k in range(4):
            wait_y(2, k)
            transpose_pairs(2, k)
            build_bd(2, k)
        for k in range(3):
            contrib(2, 0, 8, 1, k)
            tile2(k)

    ls.wait()
    for cp in lp:
        cp.wait()
    lp1.wait()
    arrival(slabs.at[sib], sib_sem.at[sib])
    for m, o, k in all_pieces:
        s = seat(m, o, k)
        arrival(slab_dst(s, 1 - c), sib_sem.at[s])
    exchange(0, 0, 8)
    exchange(1, 0, 6)
    for k in range(3):
        return1(k)

    tile1(3)

    @pl.when(heavy)
    def _():
        for b in range(4):
            contrib(2, 2 * b, 2, 1, 3)
            rsend[1, 2 * b:2 * b + 2] = acc[2, 2 * b * NPNO:(2 * b + 2) * NPNO, :].astype(BF16).reshape(2, NPNO, NPNO)
            sent_pred2.append(back2(b))
            sent_pred2[-1]().start()
        tile2(3)

    exchange(1, 6, 2)
    return1(3)

    for k in range(4):
        two = pl.ds(2 * k, 2)
        arrival(rin.at[0, two], r_sem.at[0, k])
        mine = acc[0, 2 * k * NPNO:(2 * k + 2) * NPNO, :].reshape(2, NPNO, NPNO)
        out_ref[2 * k:2 * k + 2] = mine + rin[0, 2 * k:2 * k + 2].astype(F32)

    @pl.when(sender2)
    def _():
        for k in range(4):
            two = pl.ds(2 * k, 2)
            arrival(rin.at[1, two], r_sem.at[1, k])
            out_ref[2 * k:2 * k + 2] += rin[1, 2 * k:2 * k + 2].astype(F32)
        for cp in sent_pred:
            cp().wait_send()

    @pl.when(heavy)
    def _():
        for cp in sent_pred2:
            cp().wait_send()

    for cp in sent:
        cp().wait_send()


def on_device(slab, owner, orbs, bases, amps, coupled, coupled_len):
    any_ = pl.BlockSpec(memory_space=pl.ANY)
    dma = pltpu.SemaphoreType.DMA
    return pl.pallas_call(
        kernel,
        out_shape=jax.ShapeDtypeStruct((PDEV, NPNO, NPNO), F32),
        in_specs=[any_] * 7,
        out_specs=pl.BlockSpec(memory_space=pltpu.VMEM),
        scratch_shapes=[
            pltpu.VMEM((3, PDEV, NORB, NPNO), BF16),
            pltpu.VMEM((3, PDEV, NPNO, NPNO), BF16),
            pltpu.VMEM((3, PDEV, 32), jnp.int32),
            pltpu.VMEM((3, PDEV, 32), jnp.int32),
            pltpu.VMEM((2, PDEV), jnp.int32),
            pltpu.VMEM((2, PDEV), jnp.int32),
            pltpu.SMEM((3, PDEV), jnp.int32),
            pltpu.SMEM((2, 2, PDEV), jnp.int32),
            pltpu.SMEM((32,), jnp.int32),
            pltpu.VMEM((32, HALF, NORB), BF16),
            pltpu.VMEM((3, PDEV * NPNO, NORB), BF16),
            pltpu.VMEM((3, 4, 2 * NPNO, 2 * NPNO), BF16),
            pltpu.VMEM((3, PDEV * NPNO, NPNO), F32),
            pltpu.VMEM((2, PDEV, NPNO, NPNO), BF16),
            pltpu.VMEM((2, PDEV, NPNO, NPNO), BF16),
            dma((110,)),
            dma((2, 4, 2)),
            dma((2, 3)),
            dma((2, 4)),
            dma((32,)),
            dma((32,)),
            dma((10,)),
        ],
        compiler_params=pltpu.CompilerParams(
            collective_id=0, has_side_effects=True, vmem_limit_bytes=56 * 1024 * 1024),
        name="residual",
    )(slab[0], bases, amps, coupled, coupled_len, orbs.T, owner)


def solution(mesh):
    pair = ("grp", "dev")
    in_specs = (
        P("dev", None, None), P(), P(pair, None), P(pair, None, None),
        P(pair, None, None), P(pair, None), P(pair),
    )
    return jax.shard_map(
        on_device, mesh=mesh, in_specs=in_specs, out_specs=P(pair, None, None), check_vma=False)
```

```python
import math

import jax
import jax.numpy as jnp
from jax import lax
from jax.experimental import pallas as pl
from jax.experimental.pallas import tpu as pltpu
from jax.sharding import PartitionSpec as P

NAUX, NORB, NPNO = 512, 512, 128
PDEV, NGRP = 8, 4
RING = 4
HALF = NAUX // 2
QUART = NAUX // 4
MESH = pl.DeviceIdType.MESH
BF16, F32 = jnp.bfloat16, jnp.float32
NT = (((1,), (1,)), ((), ()))


def mm(a, b, dims=None):
    if dims is None:
        return jnp.dot(a, b, preferred_element_type=F32)
    return lax.dot_general(a, b, dims, preferred_element_type=F32)


def kernel(
    slab_hbm, u_hbm, t_hbm, cpl_hbm, len_hbm, orb_hbm, owner_hbm, out_ref,
    ubuf, tbuf, meta, cpl, lenv, orbv, lens, orbs, owner, slabs, vbuf, bd, acc, halves, rsend, rin,
    send_sem, y_sem, ym_sem, r_sem, net_sem, sib_sem, loc_sem,
):
    g = lax.axis_index("grp")
    d = lax.axis_index("dev")
    rem, div = lax.rem, lax.div
    c = rem(d, 2)
    x = rem(div(d, 2), RING)
    z = div(d, 2 * RING)
    up, dn = rem(g + 1, NGRP), rem(g + NGRP - 1, NGRP)
    half = rem(g, 2)
    sender2 = div(g, 2) == c
    heavy = div(up, 2) == c
    first = div(rem(up + 1, NGRP), 2) == c

    def dev(zz, xx, cc):
        return rem(zz, RING) * (2 * RING) + rem(xx, RING) * 2 + cc

    def seat(m, o, cc):
        zz = z + (m + (o - m) * c) + RING
        xx = x + (o + (m - o) * c) + RING
        return dev(zz, xx, cc)

    sib = dev(z, x, 1 - c)

    barrier = pltpu.get_barrier_semaphore()
    partners = [(up, d), (dn, d), (g, sib)]
    for dz, dx in ((1, 0), (-1, 0), (0, 1), (0, -1)):
        for cc in (0, 1):
            partners.append((g, dev(z + dz + RING, x + dx + RING, cc)))
    for pg, pd in partners:
        pl.semaphore_signal(barrier, inc=1, device_id=(pg, pd), device_id_type=MESH)


    def local(src, dst, i):
        cp = pltpu.make_async_copy(src, dst, loc_sem.at[i])
        cp.start()
        return cp

    my_rows = slab_hbm.at[pl.ds(half * HALF, HALF), :]
    ls = local(my_rows, slabs.at[d], 4)
    lu = local(u_hbm, ubuf.at[0], 0)
    lt = local(t_hbm, tbuf.at[0], 1)
    lm = [local(cpl_hbm, cpl.at[0], 2), local(len_hbm, lens.at[0], 3)]
    lp = [local(orb_hbm, orbs.at[0], 5), local(owner_hbm, owner, 6)]
    ls.wait()
    pl.semaphore_wait(barrier, len(partners))

    sent, sent_pred = [], []
    counter = [0]

    def make(refs, pg, pd):
        i = counter[0]
        counter[0] += 1

        def build():
            src, dst, recv = refs()
            return pltpu.make_async_remote_copy(
                src_ref=src, dst_ref=dst, send_sem=send_sem.at[i], recv_sem=recv,
                device_id=(pg, pd), device_id_type=MESH)
        return build

    def push(src, dst, recv, pg, pd):
        cp = make(lambda: (src, dst, recv), pg, pd)
        cp().start()
        sent.append(cp)

    def arrival(dst, recv):
        pltpu.make_async_remote_copy(
            src_ref=dst, dst_ref=dst, send_sem=send_sem.at[0], recv_sem=recv,
            device_id=(up, d), device_id_type=MESH).wait_recv()

    def y_step(k, row, pg):
        two = pl.ds(2 * k, 2)
        return [
            make(lambda: (u_hbm.at[two], ubuf.at[row, two], y_sem.at[row - 1, k, 0]), pg, d),
            make(lambda: (t_hbm.at[two], tbuf.at[row, two], y_sem.at[row - 1, k, 1]), pg, d),
        ]

    y_sends = [cp for k in range(4) for cp in y_step(k, 1, up)]
    sent += y_sends

    def start_y():
        for cp in y_sends:
            cp().start()

    def slab_dst(s, q):
        return slabs.at[s, pl.ds(q * QUART, QUART), :]

    def y_meta(row, pg):
        return [
            make(lambda: (cpl_hbm, cpl.at[row], ym_sem.at[row - 1, 0]), pg, d),
            make(lambda: (len_hbm, lenv.at[row - 1], ym_sem.at[row - 1, 1]), pg, d),
        ]

    push(orb_hbm, orbv, ym_sem.at[0, 2], up, d)
    for cp in y_meta(1, up):
        cp().start()
        sent.append(cp)
    for q, nbrs in ((0, ((0, 1), (0, -1))), (1, ((1, 0), (-1, 0))), (1, ((0, 1), (0, -1))), (0, ((1, 0), (-1, 0)))):
        for dz, dx in nbrs:
            push(slab_dst(d, q), slab_dst(d, q), net_sem.at[d], g, dev(z + dz + RING, x + dx + RING, q))
    push(slabs.at[d], slabs.at[d], sib_sem.at[d], g, sib)
    pl.when(first)(start_y)

    @pl.when(sender2)
    def _():
        sent_pred.extend(y_meta(2, dn))
        for k in range(4):
            sent_pred.extend(y_step(k, 2, dn))
        for cp in sent_pred:
            cp().start()

    events = [(0, -1, 0), (0, 1, 1), (0, -1, 1), (0, 1, 0),
              (-1, 0, 0), (1, 0, 1), (-1, 0, 1), (1, 0, 0), (0, 2, 0), (0, 2, 1)]
    for o, k in ((-1, 0), (1, 1), (-1, 1), (1, 0)):
        events += [(-1, o, k), (1, o, k)]
    events += [(2, 0, 0), (2, 0, 1)]
    for o, k in ((2, 0), (2, 1)):
        events += [(-1, o, k), (1, o, k)]
    events += [(2, o, k) for o, k in ((-1, 0), (1, 1), (-1, 1), (1, 0), (2, 0), (2, 1))]
    all_pieces = list(events)

    def relay(n):
        for _ in range(min(n, len(events))):
            m, o, k = events.pop(0)
            s = seat(m, o, k)
            piece = slab_dst(s, c)
            arrival(piece, net_sem.at[s])
            if m == 0:
                if (o, k) == (-1, 0):
                    push(piece, piece, net_sem.at[s], g, seat(0, 1, c))
                if (o, k) == (1, 1):
                    push(piece, piece, net_sem.at[s], g, seat(0, -1, c))
                push(piece, piece, net_sem.at[s], g, seat(1, 0, c))
                push(piece, piece, net_sem.at[s], g, seat(-1, 0, c))
            elif (m, k) == (-1, 0):
                push(piece, piece, net_sem.at[s], g, seat(1, 0, c))
            elif (m, k) == (1, 1):
                push(piece, piece, net_sem.at[s], g, seat(-1, 0, c))
            push(piece, piece, sib_sem.at[s], g, sib)

    def transpose_pairs(row, j):
        for p in (2 * j, 2 * j + 1):
            vbuf[row, p] = ubuf[row, p].T

    def build_bd(row, j):
        zero = jnp.zeros((NPNO, NPNO), BF16)
        top = jnp.concatenate([tbuf[row, 2 * j], zero], axis=1)
        bot = jnp.concatenate([zero, tbuf[row, 2 * j + 1]], axis=1)
        bd[row, j] = jnp.concatenate([top, bot], axis=0)

    def count(row, cand):
        hit = jnp.sum(jnp.where(meta[row] == cand, 4.0, 0.0), axis=1, keepdims=True)
        return jnp.broadcast_to(hit, (PDEV, NPNO))

    def group_of(row):
        return (g, dn, up)[row]

    def contrib(tgt, lo, n, src, j):
        uq = jnp.concatenate([ubuf[src, 2 * j], ubuf[src, 2 * j + 1]], axis=1)
        bdq = bd[src, j]
        cand = group_of(src) * PDEV + 2 * j
        w = jnp.concatenate([count(tgt, cand), count(tgt, cand + 1)], axis=1)
        for b in range(lo, lo + n, 2):
            s = mm(vbuf[tgt, b:b + 2].reshape(2 * NPNO, NORB), uq).astype(BF16)
            proj = mm(s, bdq)
            for i in (0, 1):
                part = slice(i * NPNO, (i + 1) * NPNO)
                pw = (proj[part] * w[b + i:b + i + 1]).astype(BF16)
                acc[tgt, b + i] += mm(pw, s[part], NT)

    def contrib_pair(k, src):
        lo = 2 * k
        us = jnp.concatenate([ubuf[src, i] for i in range(PDEV)], axis=1)
        s = mm(vbuf[1, lo:lo + 2].reshape(2 * NPNO, NORB), us).astype(BF16)
        scaled = []
        for j in range(4):
            cand = group_of(src) * PDEV + 2 * j
            w = jnp.concatenate([count(1, cand), count(1, cand + 1)], axis=1)
            proj = mm(s[:, j * 256:(j + 1) * 256], bd[src, j])
            scaled.append([(proj[i * NPNO:(i + 1) * NPNO] * w[lo + i:lo + i + 1]).astype(BF16) for i in (0, 1)])
        for i in (0, 1):
            pw = jnp.concatenate([v[i] for v in scaled], axis=1)
            acc[1, lo + i] += mm(pw, s[i * NPNO:(i + 1) * NPNO], NT)

    def loop(n, fn):
        lax.fori_loop(0, n, lambda j, carry: (fn(j), carry)[1], 0)

    def exchange(row, lo, n):
        def half(t, carry):
            halves[0, t] = mm(vbuf[row, t], slabs[owner[orbs[row, 0, t]]], NT).astype(BF16)
            halves[1, t] = mm(slabs[owner[orbs[row, 1, t]]], ubuf[row, t]).astype(BF16).T
            return carry
        lax.fori_loop(lo, lo + n, half, 0)
        for t in range(lo, lo + n):
            acc[row, t] += mm(halves[0, t], halves[1, t], NT) * (1.0 / math.sqrt(NAUX))

    def wait_y(row, k):
        two = pl.ds(2 * k, 2)
        arrival(ubuf.at[row, two], y_sem.at[row - 1, k, 0])
        arrival(tbuf.at[row, two], y_sem.at[row - 1, k, 1])

    def take_meta(row):
        rows = lax.broadcasted_iota(jnp.int32, (PDEV, 32), 0)
        used = jnp.zeros((PDEV, 32), jnp.int32)
        for p in range(PDEV):
            used = jnp.where(rows == p, lens[row, p], used)
        slot = lax.broadcasted_iota(jnp.int32, (PDEV, 32), 1)
        meta[row] = jnp.where(slot < used, cpl[row], -1)

    def arrive_meta(row):
        arrival(cpl.at[row], ym_sem.at[row - 1, 0])
        arrival(lenv.at[row - 1], ym_sem.at[row - 1, 1])
        cp = pltpu.make_async_copy(lenv.at[row - 1], lens.at[row], loc_sem.at[6 + row])
        cp.start()
        cp.wait()
        take_meta(row)

    acc[...] = jnp.zeros_like(acc)
    lu.wait()
    lt.wait()
    for j in range(4):
        transpose_pairs(0, j)
        build_bd(0, j)
    for cp in lm:
        cp.wait()
    take_meta(0)
    relay(4)
    loop(4, lambda j: contrib(0, 0, 8, 0, j))
    relay(6)
    pl.when(jnp.logical_not(first))(start_y)
    arrive_meta(1)
    arrival(orbv, ym_sem.at[0, 2])
    lp1 = pltpu.make_async_copy(orbv, orbs.at[1], loc_sem.at[9])
    lp1.start()

    def tile1(k):
        wait_y(1, k)
        transpose_pairs(1, k)
        build_bd(1, k)
        contrib_pair(k, 0)

    def return1(k):
        two = pl.ds(2 * k, 2)
        rsend[0, 2 * k:2 * k + 2] = acc[1, 2 * k:2 * k + 2].astype(BF16)
        return make(lambda: (rsend.at[0, two], rin.at[0, two], r_sem.at[0, k]), dn, d)

    def return2(b):
        two = pl.ds(2 * b, 2)
        rsend[1, 2 * b:2 * b + 2] = acc[2, 2 * b:2 * b + 2].astype(BF16)
        return make(lambda: (rsend.at[1, two], rin.at[1, two], r_sem.at[1, b]), up, d)

    def go(cps, cp):
        cp().start()
        cps.append(cp)

    def wait_slabs():
        for cp in lp:
            cp.wait()
        lp1.wait()
        arrival(slabs.at[sib], sib_sem.at[sib])
        for m, o, k in all_pieces:
            s = seat(m, o, k)
            arrival(slab_dst(s, 1 - c), sib_sem.at[s])

    common_sent, common_events, common_count = sent[:], events[:], counter[0]

    @pl.when(heavy)
    def _():
        sent[:], events[:] = [], common_events[:]
        cps = []
        for k in range(4):
            tile1(k)
            relay(2)
            contrib(0, 0, 8, 1, k)
            relay(2)
        arrive_meta(2)
        for k in range(4):
            wait_y(2, k)
            transpose_pairs(2, k)
            build_bd(2, k)
        relay(2)
        for k in range(4):
            contrib(2, 0, 8, 1, k)
            relay(1)
        for b in range(4):
            go(cps, return2(b))
        for k in range(4):
            contrib_pair(k, 2)
            relay(30 if k == 3 else 1)
        wait_slabs()
        exchange(1, 0, 8)
        for k in range(4):
            go(cps, return1(k))
        exchange(0, 0, 8)
        for cp in cps + sent:
            cp().wait_send()

    counter[0] = common_count

    @pl.when(jnp.logical_not(heavy))
    def _():
        sent[:], events[:] = [], common_events[:]
        cps = []
        relay(30)
        wait_slabs()
        exchange(0, 0, 8)
        for k in range(4):
            tile1(k)
            exchange(1, 2 * k, 2)
            go(cps, return1(k))
            contrib(0, 0, 8, 1, k)
        for cp in cps + sent:
            cp().wait_send()

    sent[:] = common_sent

    for k in range(4):
        two = pl.ds(2 * k, 2)
        arrival(rin.at[0, two], r_sem.at[0, k])
        mine = acc[0, 2 * k:2 * k + 2]
        out_ref[2 * k:2 * k + 2] = mine + rin[0, 2 * k:2 * k + 2].astype(F32)

    @pl.when(sender2)
    def _():
        for k in range(4):
            two = pl.ds(2 * k, 2)
            arrival(rin.at[1, two], r_sem.at[1, k])
            out_ref[2 * k:2 * k + 2] += rin[1, 2 * k:2 * k + 2].astype(F32)
        for cp in sent_pred:
            cp().wait_send()

    for cp in sent:
        cp().wait_send()


def on_device(slab, owner, orbs, bases, amps, coupled, coupled_len):
    any_ = pl.BlockSpec(memory_space=pl.ANY)
    dma = pltpu.SemaphoreType.DMA
    return pl.pallas_call(
        kernel,
        out_shape=jax.ShapeDtypeStruct((PDEV, NPNO, NPNO), F32),
        in_specs=[any_] * 7,
        out_specs=pl.BlockSpec(memory_space=pltpu.VMEM),
        scratch_shapes=[
            pltpu.VMEM((3, PDEV, NORB, NPNO), BF16),
            pltpu.VMEM((3, PDEV, NPNO, NPNO), BF16),
            pltpu.VMEM((3, PDEV, 32), jnp.int32),
            pltpu.VMEM((3, PDEV, 32), jnp.int32),
            pltpu.VMEM((2, PDEV), jnp.int32),
            pltpu.VMEM((2, PDEV), jnp.int32),
            pltpu.SMEM((3, PDEV), jnp.int32),
            pltpu.SMEM((2, 2, PDEV), jnp.int32),
            pltpu.SMEM((32,), jnp.int32),
            pltpu.VMEM((32, HALF, NORB), BF16),
            pltpu.VMEM((3, PDEV, NPNO, NORB), BF16),
            pltpu.VMEM((3, 4, 2 * NPNO, 2 * NPNO), BF16),
            pltpu.VMEM((3, PDEV, NPNO, NPNO), F32),
            pltpu.VMEM((2, PDEV, NPNO, HALF), BF16),
            pltpu.VMEM((2, PDEV, NPNO, NPNO), BF16),
            pltpu.VMEM((2, PDEV, NPNO, NPNO), BF16),
            dma((110,)),
            dma((2, 4, 2)),
            dma((2, 3)),
            dma((2, 4)),
            dma((32,)),
            dma((32,)),
            dma((10,)),
        ],
        compiler_params=pltpu.CompilerParams(
            collective_id=0, has_side_effects=True, vmem_limit_bytes=56 * 1024 * 1024),
        name="residual",
    )(slab[0], bases, amps, coupled, coupled_len, orbs.T, owner)


def solution(mesh):
    pair = ("grp", "dev")
    in_specs = (
        P("dev", None, None), P(), P(pair, None), P(pair, None, None),
        P(pair, None, None), P(pair, None), P(pair),
    )
    return jax.shard_map(
        on_device, mesh=mesh, in_specs=in_specs, out_specs=P(pair, None, None), check_vma=False)
```

```python
import math

import jax
import jax.numpy as jnp
from jax import lax
from jax.experimental import pallas as pl
from jax.experimental.pallas import tpu as pltpu
from jax.sharding import PartitionSpec as P

NAUX, NORB, NPNO = 512, 512, 128
PDEV, NGRP = 8, 4
RING = 4
HALF = NAUX // 2
QUART = NAUX // 4
STEPS = ((0, 2), (2, 2), (4, 2), (6, 1), (7, 1))
MESH = pl.DeviceIdType.MESH
BF16, F32 = jnp.bfloat16, jnp.float32
TN = (((0,), (0,)), ((), ()))
NT = (((1,), (1,)), ((), ()))


def mm(a, b, dims=None):
    if dims is None:
        return jnp.dot(a, b, preferred_element_type=F32)
    return lax.dot_general(a, b, dims, preferred_element_type=F32)


def kernel(
    slab_hbm, u_hbm, t_hbm, cpl_hbm, len_hbm, orb_hbm, owner_hbm, own_out, rin1, rin2,
    ubuf, tbuf, meta, cpl, lenv, orbv, lens, orbs, owner, slabs, vbuf, bd, acc, halves, rsend,
    send_sem, y_sem, ym_sem, r_sem, net_sem, sib_sem, loc_sem,
):
    g = lax.axis_index("grp")
    d = lax.axis_index("dev")
    rem, div = lax.rem, lax.div
    c = rem(d, 2)
    x = rem(div(d, 2), RING)
    z = div(d, 2 * RING)
    up, dn = rem(g + 1, NGRP), rem(g + NGRP - 1, NGRP)
    half = rem(g, 2)
    sender2 = div(g, 2) == c
    heavy = div(up, 2) == c
    first = div(rem(up + 1, NGRP), 2) == c

    def dev(zz, xx, cc):
        return rem(zz, RING) * (2 * RING) + rem(xx, RING) * 2 + cc

    def seat(m, o, cc):
        zz = z + (m + (o - m) * c) + RING
        xx = x + (o + (m - o) * c) + RING
        return dev(zz, xx, cc)

    sib = dev(z, x, 1 - c)

    barrier = pltpu.get_barrier_semaphore()
    partners = [(up, d), (dn, d), (g, sib)]
    for dz, dx in ((1, 0), (-1, 0), (0, 1), (0, -1)):
        for cc in (0, 1):
            partners.append((g, dev(z + dz + RING, x + dx + RING, cc)))
    for pg, pd in partners:
        pl.semaphore_signal(barrier, inc=1, device_id=(pg, pd), device_id_type=MESH)


    def local(src, dst, i):
        cp = pltpu.make_async_copy(src, dst, loc_sem.at[i])
        cp.start()
        return cp

    my_rows = slab_hbm.at[pl.ds(half * HALF, HALF), :]
    ls = local(my_rows, slabs.at[d], 4)
    lu = local(u_hbm, ubuf.at[0], 0)
    lt = local(t_hbm, tbuf.at[0], 1)
    lm = [local(cpl_hbm, cpl.at[0], 2), local(len_hbm, lens.at[0], 3)]
    lp = [local(orb_hbm, orbs.at[0], 5), local(owner_hbm, owner, 6)]
    ls.wait()
    pl.semaphore_wait(barrier, len(partners))

    sent, sent_pred = [], []
    counter = [0]

    def make(refs, pg, pd):
        i = counter[0]
        counter[0] += 1

        def build():
            src, dst, recv = refs()
            return pltpu.make_async_remote_copy(
                src_ref=src, dst_ref=dst, send_sem=send_sem.at[i], recv_sem=recv,
                device_id=(pg, pd), device_id_type=MESH)
        return build

    def push(src, dst, recv, pg, pd):
        cp = make(lambda: (src, dst, recv), pg, pd)
        cp().start()
        sent.append(cp)

    def arrival(dst, recv):
        pltpu.make_async_remote_copy(
            src_ref=dst, dst_ref=dst, send_sem=send_sem.at[0], recv_sem=recv,
            device_id=(up, d), device_id_type=MESH).wait_recv()

    def y_step(k, row, pg):
        two = pl.ds(*STEPS[k])
        return [
            make(lambda: (u_hbm.at[two], ubuf.at[row, two], y_sem.at[row - 1, k, 0]), pg, d),
            make(lambda: (t_hbm.at[two], tbuf.at[row, two], y_sem.at[row - 1, k, 1]), pg, d),
        ]

    y_sends = [cp for k in range(len(STEPS)) for cp in y_step(k, 1, up)]
    sent += y_sends

    def start_y():
        for cp in y_sends:
            cp().start()

    def slab_dst(s, q):
        return slabs.at[s, pl.ds(q * QUART, QUART), :]

    def y_meta(row, pg):
        return [
            make(lambda: (cpl_hbm, cpl.at[row], ym_sem.at[row - 1, 0]), pg, d),
            make(lambda: (len_hbm, lenv.at[row - 1], ym_sem.at[row - 1, 1]), pg, d),
        ]

    push(orb_hbm, orbv, ym_sem.at[0, 2], up, d)
    for cp in y_meta(1, up):
        cp().start()
        sent.append(cp)
    for q, nbrs in ((0, ((0, 1), (0, -1))), (1, ((1, 0), (-1, 0))), (1, ((0, 1), (0, -1))), (0, ((1, 0), (-1, 0)))):
        for dz, dx in nbrs:
            push(slab_dst(d, q), slab_dst(d, q), net_sem.at[d], g, dev(z + dz + RING, x + dx + RING, q))
    push(slabs.at[d], slabs.at[d], sib_sem.at[d], g, sib)
    pl.when(first)(start_y)

    @pl.when(sender2)
    def _():
        sent_pred.extend(y_meta(2, dn))
        for k in range(len(STEPS)):
            sent_pred.extend(y_step(k, 2, dn))
        for cp in sent_pred:
            cp().start()

    events = [(0, -1, 0), (0, 1, 1), (0, -1, 1), (0, 1, 0),
              (-1, 0, 0), (1, 0, 1), (-1, 0, 1), (1, 0, 0), (0, 2, 0), (0, 2, 1)]
    for o, k in ((-1, 0), (1, 1), (-1, 1), (1, 0)):
        events += [(-1, o, k), (1, o, k)]
    events += [(2, 0, 0), (2, 0, 1)]
    for o, k in ((2, 0), (2, 1)):
        events += [(-1, o, k), (1, o, k)]
    events += [(2, o, k) for o, k in ((-1, 0), (1, 1), (-1, 1), (1, 0), (2, 0), (2, 1))]
    all_pieces = list(events)

    def relay(n):
        for _ in range(min(n, len(events))):
            m, o, k = events.pop(0)
            s = seat(m, o, k)
            piece = slab_dst(s, c)
            arrival(piece, net_sem.at[s])
            if m == 0:
                if (o, k) == (-1, 0):
                    push(piece, piece, net_sem.at[s], g, seat(0, 1, c))
                if (o, k) == (1, 1):
                    push(piece, piece, net_sem.at[s], g, seat(0, -1, c))
                push(piece, piece, net_sem.at[s], g, seat(1, 0, c))
                push(piece, piece, net_sem.at[s], g, seat(-1, 0, c))
            elif (m, k) == (-1, 0):
                push(piece, piece, net_sem.at[s], g, seat(1, 0, c))
            elif (m, k) == (1, 1):
                push(piece, piece, net_sem.at[s], g, seat(-1, 0, c))
            push(piece, piece, sib_sem.at[s], g, sib)

    def transpose_pairs(row, lo, n):
        for p in range(lo, lo + n):
            vbuf[row, p] = ubuf[row, p].T

    def build_bd(row, j):
        zero = jnp.zeros((NPNO, NPNO), BF16)
        top = jnp.concatenate([tbuf[row, 2 * j], zero], axis=1)
        bot = jnp.concatenate([zero, tbuf[row, 2 * j + 1]], axis=1)
        bd[row, j] = jnp.concatenate([top, bot], axis=0)

    def count(row, cand):
        hit = jnp.sum(jnp.where(meta[row] == cand, 4.0, 0.0), axis=1, keepdims=True)
        return jnp.broadcast_to(hit, (PDEV, NPNO))

    def group_of(row):
        return (g, dn, up)[row]

    def contrib(tgt, lo, n, src, j):
        uq = jnp.concatenate([ubuf[src, 2 * j], ubuf[src, 2 * j + 1]], axis=1)
        bdq = bd[src, j]
        cand = group_of(src) * PDEV + 2 * j
        w = jnp.concatenate([count(tgt, cand), count(tgt, cand + 1)], axis=1)
        for b in range(lo, lo + n, 2):
            s = mm(vbuf[tgt, b:b + 2].reshape(2 * NPNO, NORB), uq).astype(BF16)
            proj = mm(s, bdq)
            for i in (0, 1):
                part = slice(i * NPNO, (i + 1) * NPNO)
                pw = (proj[part] * w[b + i:b + i + 1]).astype(BF16)
                acc[tgt, b + i] += mm(pw, s[part], NT)

    def contrib_pair(lo, n, src):
        us = jnp.concatenate([ubuf[src, i] for i in range(PDEV)], axis=1)
        s = mm(vbuf[1, lo:lo + n].reshape(n * NPNO, NORB), us).astype(BF16)
        scaled = []
        for j in range(4):
            cand = group_of(src) * PDEV + 2 * j
            w = jnp.concatenate([count(1, cand), count(1, cand + 1)], axis=1)
            proj = mm(s[:, j * 256:(j + 1) * 256], bd[src, j])
            scaled.append([(proj[i * NPNO:(i + 1) * NPNO] * w[lo + i:lo + i + 1]).astype(BF16) for i in range(n)])
        for i in range(n):
            pw = jnp.concatenate([v[i] for v in scaled], axis=1)
            acc[1, lo + i] += mm(pw, s[i * NPNO:(i + 1) * NPNO], NT)

    def loop(n, fn):
        lax.fori_loop(0, n, lambda j, carry: (fn(j), carry)[1], 0)

    def exchange(row, lo, n):
        unit = next(v for v in (4, 2, 1) if n % v == 0)

        def half(b, carry):
            for i in range(unit):
                t = lo + b * unit + i
                halves[t, :HALF] = mm(slabs[owner[orbs[row, 0, t]]], ubuf[row, t]).astype(BF16)
                halves[t, HALF:] = mm(slabs[owner[orbs[row, 1, t]]], ubuf[row, t]).astype(BF16)
            return carry
        lax.fori_loop(0, n // unit, half, 0)
        for t in range(lo, lo + n):
            acc[row, t] += mm(halves[t, :HALF], halves[t, HALF:], TN) * (1.0 / math.sqrt(NAUX))

    def wait_y(row, k):
        two = pl.ds(*STEPS[k])
        arrival(ubuf.at[row, two], y_sem.at[row - 1, k, 0])
        arrival(tbuf.at[row, two], y_sem.at[row - 1, k, 1])

    def take_meta(row):
        rows = lax.broadcasted_iota(jnp.int32, (PDEV, 32), 0)
        used = jnp.zeros((PDEV, 32), jnp.int32)
        for p in range(PDEV):
            used = jnp.where(rows == p, lens[row, p], used)
        slot = lax.broadcasted_iota(jnp.int32, (PDEV, 32), 1)
        meta[row] = jnp.where(slot < used, cpl[row], -1)

    def arrive_meta(row):
        arrival(cpl.at[row], ym_sem.at[row - 1, 0])
        arrival(lenv.at[row - 1], ym_sem.at[row - 1, 1])
        cp = pltpu.make_async_copy(lenv.at[row - 1], lens.at[row], loc_sem.at[6 + row])
        cp.start()
        cp.wait()
        take_meta(row)

    acc[...] = jnp.zeros_like(acc)
    rsend[1] = jnp.zeros((PDEV, NPNO, NPNO), BF16)
    lu.wait()
    lt.wait()
    for j in range(4):
        transpose_pairs(0, 2 * j, 2)
        build_bd(0, j)
    for cp in lm:
        cp.wait()
    take_meta(0)
    loop(4, lambda j: contrib(0, 0, 8, 0, j))
    relay(12)
    pl.when(jnp.logical_not(first))(start_y)
    arrive_meta(1)
    arrival(orbv, ym_sem.at[0, 2])
    lp1 = pltpu.make_async_copy(orbv, orbs.at[1], loc_sem.at[10])
    lp1.start()

    def clear():
        return pltpu.make_async_copy(rsend.at[1], rin2, loc_sem.at[11])

    @pl.when(jnp.logical_not(sender2))
    def _():
        clear().start()
        clear().wait()

    def tile1(k):
        lo, n = STEPS[k]
        wait_y(1, k)
        transpose_pairs(1, lo, n)
        if (lo + n) % 2 == 0:
            build_bd(1, lo // 2)
        contrib_pair(lo, n, 0)

    def return1(k):
        lo, n = STEPS[k]
        rsend[0, lo:lo + n] = acc[1, lo:lo + n].astype(BF16)
        return make(lambda: (rsend.at[0, pl.ds(lo, n)], rin1.at[pl.ds(lo, n)], r_sem.at[0, k]), dn, d)

    def return2(b):
        two = pl.ds(2 * b, 2)
        rsend[1, 2 * b:2 * b + 2] = acc[2, 2 * b:2 * b + 2].astype(BF16)
        return make(lambda: (rsend.at[1, two], rin2.at[two], r_sem.at[1, b]), up, d)

    def go(cps, cp):
        cp().start()
        cps.append(cp)

    def wait_slabs():
        for cp in lp:
            cp.wait()
        lp1.wait()
        arrival(slabs.at[sib], sib_sem.at[sib])
        for m, o, k in all_pieces:
            s = seat(m, o, k)
            arrival(slab_dst(s, 1 - c), sib_sem.at[s])

    def flush():
        return pltpu.make_async_copy(acc.at[0], own_out, loc_sem.at[9])

    common_sent, common_events, common_count = sent[:], events[:], counter[0]

    @pl.when(heavy)
    def _():
        sent[:], events[:] = [], common_events[:]
        cps = []
        for k in range(5):
            tile1(k)
            relay((0, 0, 2, 2, 0)[k])
            if k < 3:
                contrib(0, 0, 8, 1, k)
                relay((0, 2, 2)[k])
        contrib(0, 0, 8, 1, 3)
        relay(2)
        arrive_meta(2)
        for k in range(5):
            wait_y(2, k)
        transpose_pairs(2, 0, PDEV)
        for j in range(4):
            build_bd(2, j)
        for k in range(4):
            contrib(2, 0, 8, 1, k)
            relay((2, 0, 2, 0)[k])
        for b in range(4):
            go(cps, return2(b))
        for k in range(4):
            contrib_pair(2 * k, 2, 2)
            relay((2, 0, 30, 0)[k])
        wait_slabs()
        exchange(1, 0, 4)
        go(cps, return1(0))
        go(cps, return1(1))
        exchange(1, 4, 4)
        for k in (2, 3, 4):
            go(cps, return1(k))
        exchange(0, 0, 8)
        flush().start()
        for cp in cps + sent:
            cp().wait_send()

    counter[0] = common_count

    @pl.when(jnp.logical_not(heavy))
    def _():
        sent[:], events[:] = [], common_events[:]
        cps = []
        relay(6)
        tile1(0)
        relay(4)
        tile1(1)
        relay(30)
        contrib(0, 0, 8, 1, 0)
        contrib(0, 0, 8, 1, 1)
        wait_slabs()
        exchange(1, 0, 4)
        go(cps, return1(0))
        go(cps, return1(1))
        exchange(0, 0, 4)
        tile1(2)
        exchange(1, 4, 2)
        go(cps, return1(2))
        for k in (3, 4):
            tile1(k)
            exchange(1, STEPS[k][0], 1)
            go(cps, return1(k))
        contrib(0, 0, 8, 1, 2)
        exchange(0, 4, 4)
        contrib(0, 0, 8, 1, 3)
        flush().start()
        for cp in cps + sent:
            cp().wait_send()

    sent[:] = common_sent

    flush().wait()
    for k, (lo, n) in enumerate(STEPS):
        arrival(rin1.at[pl.ds(lo, n)], r_sem.at[0, k])

    @pl.when(sender2)
    def _():
        for k in range(4):
            arrival(rin2.at[pl.ds(2 * k, 2)], r_sem.at[1, k])
        for cp in sent_pred:
            cp().wait_send()

    for cp in sent:
        cp().wait_send()


def on_device(slab, owner, orbs, bases, amps, coupled, coupled_len):
    any_ = pl.BlockSpec(memory_space=pl.ANY)
    dma = pltpu.SemaphoreType.DMA
    def shape(t):
        return jax.ShapeDtypeStruct((PDEV, NPNO, NPNO), t)

    own, back1, back2 = pl.pallas_call(
        kernel,
        out_shape=[shape(F32), shape(BF16), shape(BF16)],
        in_specs=[any_] * 7,
        out_specs=[any_] * 3,
        scratch_shapes=[
            pltpu.VMEM((3, PDEV, NORB, NPNO), BF16),
            pltpu.VMEM((3, PDEV, NPNO, NPNO), BF16),
            pltpu.VMEM((3, PDEV, 32), jnp.int32),
            pltpu.VMEM((3, PDEV, 32), jnp.int32),
            pltpu.VMEM((2, PDEV), jnp.int32),
            pltpu.VMEM((2, PDEV), jnp.int32),
            pltpu.SMEM((3, PDEV), jnp.int32),
            pltpu.SMEM((2, 2, PDEV), jnp.int32),
            pltpu.SMEM((32,), jnp.int32),
            pltpu.VMEM((32, HALF, NORB), BF16),
            pltpu.VMEM((3, PDEV, NPNO, NORB), BF16),
            pltpu.VMEM((3, 4, 2 * NPNO, 2 * NPNO), BF16),
            pltpu.VMEM((3, PDEV, NPNO, NPNO), F32),
            pltpu.VMEM((PDEV, NAUX, NPNO), BF16),
            pltpu.VMEM((2, PDEV, NPNO, NPNO), BF16),
            dma((120,)),
            dma((2, 5, 2)),
            dma((2, 3)),
            dma((2, 5)),
            dma((32,)),
            dma((32,)),
            dma((12,)),
        ],
        compiler_params=pltpu.CompilerParams(
            collective_id=0, has_side_effects=True, vmem_limit_bytes=56 * 1024 * 1024),
        name="residual",
    )(slab[0], bases, amps, coupled, coupled_len, orbs.T, owner)
    return own + back1.astype(F32) + back2.astype(F32)


def solution(mesh):
    pair = ("grp", "dev")
    in_specs = (
        P("dev", None, None), P(), P(pair, None), P(pair, None, None),
        P(pair, None, None), P(pair, None), P(pair),
    )
    return jax.shard_map(
        on_device, mesh=mesh, in_specs=in_specs, out_specs=P(pair, None, None), check_vma=False)
```

```python
import math

import jax
import jax.numpy as jnp
from jax import lax
from jax.experimental import pallas as pl
from jax.experimental.pallas import tpu as pltpu
from jax.sharding import PartitionSpec as P

NAUX, NORB, NPNO = 512, 512, 128
PDEV, NGRP = 8, 4
RING = 4
HALF = NAUX // 2
QUART = NAUX // 4
STEPS = ((0, 2), (2, 2), (4, 2), (6, 1), (7, 1))
MESH = pl.DeviceIdType.MESH
BF16, F32 = jnp.bfloat16, jnp.float32
TN = (((0,), (0,)), ((), ()))
NT = (((1,), (1,)), ((), ()))


def mm(a, b, dims=None):
    if dims is None:
        return jnp.dot(a, b, preferred_element_type=F32)
    return lax.dot_general(a, b, dims, preferred_element_type=F32)


def kernel(
    slab_hbm, u_hbm, t_hbm, cpl_hbm, len_hbm, orb_hbm, owner_hbm, own_out, rin1, rin2,
    ubuf, tbuf, meta, cpl, lenv, orbv, lens, orbs, owner, slabs, vbuf, bd, acc, halves, rsend,
    send_sem, y_sem, ym_sem, r_sem, net_sem, sib_sem, loc_sem,
):
    g = lax.axis_index("grp")
    d = lax.axis_index("dev")
    rem, div = lax.rem, lax.div
    c = rem(d, 2)
    x = rem(div(d, 2), RING)
    z = div(d, 2 * RING)
    up, dn = rem(g + 1, NGRP), rem(g + NGRP - 1, NGRP)
    half = rem(g, 2)
    sender2 = div(g, 2) == c
    heavy = div(up, 2) == c
    first = div(rem(up + 1, NGRP), 2) == c

    def dev(zz, xx, cc):
        return rem(zz, RING) * (2 * RING) + rem(xx, RING) * 2 + cc

    def seat(m, o, cc):
        zz = z + (m + (o - m) * c) + RING
        xx = x + (o + (m - o) * c) + RING
        return dev(zz, xx, cc)

    sib = dev(z, x, 1 - c)

    barrier = pltpu.get_barrier_semaphore()
    partners = [(up, d), (dn, d), (g, sib)]
    for dz, dx in ((1, 0), (-1, 0), (0, 1), (0, -1)):
        for cc in (0, 1):
            partners.append((g, dev(z + dz + RING, x + dx + RING, cc)))
    for pg, pd in partners:
        pl.semaphore_signal(barrier, inc=1, device_id=(pg, pd), device_id_type=MESH)


    def local(src, dst, i):
        cp = pltpu.make_async_copy(src, dst, loc_sem.at[i])
        cp.start()
        return cp

    my_rows = slab_hbm.at[pl.ds(half * HALF, HALF), :]
    ls = local(my_rows, slabs.at[d], 4)
    lu = local(u_hbm, ubuf.at[0], 0)
    lt = local(t_hbm, tbuf.at[0], 1)
    lm = [local(cpl_hbm, cpl.at[0], 2), local(len_hbm, lens.at[0], 3)]
    lp = [local(orb_hbm, orbs.at[0], 5), local(owner_hbm, owner, 6)]
    ls.wait()
    pl.semaphore_wait(barrier, len(partners))

    sent, sent_pred = [], []
    counter = [0]

    def make(refs, pg, pd):
        i = counter[0]
        counter[0] += 1

        def build():
            src, dst, recv = refs()
            return pltpu.make_async_remote_copy(
                src_ref=src, dst_ref=dst, send_sem=send_sem.at[i], recv_sem=recv,
                device_id=(pg, pd), device_id_type=MESH)
        return build

    def push(src, dst, recv, pg, pd):
        cp = make(lambda: (src, dst, recv), pg, pd)
        cp().start()
        sent.append(cp)

    def arrival(dst, recv):
        pltpu.make_async_remote_copy(
            src_ref=dst, dst_ref=dst, send_sem=send_sem.at[0], recv_sem=recv,
            device_id=(up, d), device_id_type=MESH).wait_recv()

    def y_step(k, row, pg):
        two = pl.ds(*STEPS[k])
        return [
            make(lambda: (u_hbm.at[two], ubuf.at[row, two], y_sem.at[row - 1, k, 0]), pg, d),
            make(lambda: (t_hbm.at[two], tbuf.at[row, two], y_sem.at[row - 1, k, 1]), pg, d),
        ]

    y_sends = [cp for k in range(len(STEPS)) for cp in y_step(k, 1, up)]
    sent += y_sends

    def start_y():
        for cp in y_sends:
            cp().start()

    def slab_dst(s, q):
        return slabs.at[s, pl.ds(q * QUART, QUART), :]

    def y_meta(row, pg):
        return [
            make(lambda: (cpl_hbm, cpl.at[row], ym_sem.at[row - 1, 0]), pg, d),
            make(lambda: (len_hbm, lenv.at[row - 1], ym_sem.at[row - 1, 1]), pg, d),
        ]

    push(orb_hbm, orbv, ym_sem.at[0, 2], up, d)
    for cp in y_meta(1, up):
        cp().start()
        sent.append(cp)
    pl.when(first)(start_y)

    @pl.when(sender2)
    def _():
        sent_pred.extend(y_meta(2, dn))
        for k in range(len(STEPS)):
            sent_pred.extend(y_step(k, 2, dn))
        for cp in sent_pred:
            cp().start()

    for q, nbrs in ((0, ((0, 1), (0, -1))), (1, ((1, 0), (-1, 0))), (1, ((0, 1), (0, -1))), (0, ((1, 0), (-1, 0)))):
        for dz, dx in nbrs:
            push(slab_dst(d, q), slab_dst(d, q), net_sem.at[d], g, dev(z + dz + RING, x + dx + RING, q))
    push(slabs.at[d], slabs.at[d], sib_sem.at[d], g, sib)

    events = [(0, -1, 0), (0, 1, 1), (0, -1, 1), (0, 1, 0),
              (-1, 0, 0), (1, 0, 1), (-1, 0, 1), (1, 0, 0), (0, 2, 0), (0, 2, 1)]
    for o, k in ((-1, 0), (1, 1), (-1, 1), (1, 0)):
        events += [(-1, o, k), (1, o, k)]
    events += [(2, 0, 0), (2, 0, 1)]
    for o, k in ((2, 0), (2, 1)):
        events += [(-1, o, k), (1, o, k)]
    events += [(2, o, k) for o, k in ((-1, 0), (1, 1), (-1, 1), (1, 0), (2, 0), (2, 1))]
    all_pieces = list(events)

    def relay(n):
        for _ in range(min(n, len(events))):
            m, o, k = events.pop(0)
            s = seat(m, o, k)
            piece = slab_dst(s, c)
            arrival(piece, net_sem.at[s])
            if m == 0:
                if (o, k) == (-1, 0):
                    push(piece, piece, net_sem.at[s], g, seat(0, 1, c))
                if (o, k) == (1, 1):
                    push(piece, piece, net_sem.at[s], g, seat(0, -1, c))
                push(piece, piece, net_sem.at[s], g, seat(1, 0, c))
                push(piece, piece, net_sem.at[s], g, seat(-1, 0, c))
            elif (m, k) == (-1, 0):
                push(piece, piece, net_sem.at[s], g, seat(1, 0, c))
            elif (m, k) == (1, 1):
                push(piece, piece, net_sem.at[s], g, seat(-1, 0, c))
            push(piece, piece, sib_sem.at[s], g, sib)

    def transpose_pairs(row, lo, n):
        for p in range(lo, lo + n):
            vbuf[row, p] = ubuf[row, p].T

    def build_bd(row, j):
        zero = jnp.zeros((NPNO, NPNO), BF16)
        top = jnp.concatenate([tbuf[row, 2 * j], zero], axis=1)
        bot = jnp.concatenate([zero, tbuf[row, 2 * j + 1]], axis=1)
        bd[row, j] = jnp.concatenate([top, bot], axis=0)

    def count(row, cand):
        hit = jnp.sum(jnp.where(meta[row] == cand, 4.0, 0.0), axis=1, keepdims=True)
        return jnp.broadcast_to(hit, (PDEV, NPNO))

    def group_of(row):
        return (g, dn, up)[row]

    def contrib(tgt, lo, n, src, j):
        uq = jnp.concatenate([ubuf[src, 2 * j], ubuf[src, 2 * j + 1]], axis=1)
        bdq = bd[src, j]
        cand = group_of(src) * PDEV + 2 * j
        w = jnp.concatenate([count(tgt, cand), count(tgt, cand + 1)], axis=1)
        for b in range(lo, lo + n, 2):
            s = mm(vbuf[tgt, b:b + 2].reshape(2 * NPNO, NORB), uq).astype(BF16)
            proj = mm(s, bdq)
            for i in (0, 1):
                part = slice(i * NPNO, (i + 1) * NPNO)
                pw = (proj[part] * w[b + i:b + i + 1]).astype(BF16)
                acc[tgt, b + i] += mm(pw, s[part], NT)

    def contrib_pair(lo, n, src):
        us = jnp.concatenate([ubuf[src, i] for i in range(PDEV)], axis=1)
        s = mm(vbuf[1, lo:lo + n].reshape(n * NPNO, NORB), us).astype(BF16)
        scaled = []
        for j in range(4):
            cand = group_of(src) * PDEV + 2 * j
            w = jnp.concatenate([count(1, cand), count(1, cand + 1)], axis=1)
            proj = mm(s[:, j * 256:(j + 1) * 256], bd[src, j])
            scaled.append([(proj[i * NPNO:(i + 1) * NPNO] * w[lo + i:lo + i + 1]).astype(BF16) for i in range(n)])
        for i in range(n):
            pw = jnp.concatenate([v[i] for v in scaled], axis=1)
            acc[1, lo + i] += mm(pw, s[i * NPNO:(i + 1) * NPNO], NT)

    def loop(n, fn):
        lax.fori_loop(0, n, lambda j, carry: (fn(j), carry)[1], 0)

    def exchange(row, lo, n):
        unit = next(v for v in (4, 2, 1) if n % v == 0)

        def half(b, carry):
            for i in range(unit):
                t = lo + b * unit + i
                halves[t, :HALF] = mm(slabs[owner[orbs[row, 0, t]]], ubuf[row, t]).astype(BF16)
                halves[t, HALF:] = mm(slabs[owner[orbs[row, 1, t]]], ubuf[row, t]).astype(BF16)
            return carry
        lax.fori_loop(0, n // unit, half, 0)
        for t in range(lo, lo + n):
            acc[row, t] += mm(halves[t, :HALF], halves[t, HALF:], TN) * (1.0 / math.sqrt(NAUX))

    def wait_y(row, k):
        two = pl.ds(*STEPS[k])
        arrival(ubuf.at[row, two], y_sem.at[row - 1, k, 0])
        arrival(tbuf.at[row, two], y_sem.at[row - 1, k, 1])

    def take_meta(row):
        rows = lax.broadcasted_iota(jnp.int32, (PDEV, 32), 0)
        used = jnp.zeros((PDEV, 32), jnp.int32)
        for p in range(PDEV):
            used = jnp.where(rows == p, lens[row, p], used)
        slot = lax.broadcasted_iota(jnp.int32, (PDEV, 32), 1)
        meta[row] = jnp.where(slot < used, cpl[row], -1)

    def arrive_meta(row):
        arrival(cpl.at[row], ym_sem.at[row - 1, 0])
        arrival(lenv.at[row - 1], ym_sem.at[row - 1, 1])
        cp = pltpu.make_async_copy(lenv.at[row - 1], lens.at[row], loc_sem.at[6 + row])
        cp.start()
        cp.wait()
        take_meta(row)

    acc[...] = jnp.zeros_like(acc)
    rsend[1] = jnp.zeros((PDEV, NPNO, NPNO), BF16)
    lu.wait()
    lt.wait()
    for j in range(4):
        transpose_pairs(0, 2 * j, 2)
        build_bd(0, j)
    for cp in lm:
        cp.wait()
    take_meta(0)
    loop(4, lambda j: contrib(0, 0, 8, 0, j))
    relay(12)
    pl.when(jnp.logical_not(first))(start_y)
    arrive_meta(1)
    arrival(orbv, ym_sem.at[0, 2])
    lp1 = pltpu.make_async_copy(orbv, orbs.at[1], loc_sem.at[10])
    lp1.start()

    def clear():
        return pltpu.make_async_copy(rsend.at[1], rin2, loc_sem.at[11])

    @pl.when(jnp.logical_not(sender2))
    def _():
        clear().start()
        clear().wait()

    def tile1(k):
        lo, n = STEPS[k]
        wait_y(1, k)
        transpose_pairs(1, lo, n)
        if (lo + n) % 2 == 0:
            build_bd(1, lo // 2)
        contrib_pair(lo, n, 0)

    def return1(k):
        lo, n = STEPS[k]
        rsend[0, lo:lo + n] = acc[1, lo:lo + n].astype(BF16)
        return make(lambda: (rsend.at[0, pl.ds(lo, n)], rin1.at[pl.ds(lo, n)], r_sem.at[0, k]), dn, d)

    def return2(b):
        two = pl.ds(2 * b, 2)
        rsend[1, 2 * b:2 * b + 2] = acc[2, 2 * b:2 * b + 2].astype(BF16)
        return make(lambda: (rsend.at[1, two], rin2.at[two], r_sem.at[1, b]), up, d)

    def go(cps, cp):
        cp().start()
        cps.append(cp)

    def wait_slabs():
        for cp in lp:
            cp.wait()
        lp1.wait()
        arrival(slabs.at[sib], sib_sem.at[sib])
        for m, o, k in all_pieces:
            s = seat(m, o, k)
            arrival(slab_dst(s, 1 - c), sib_sem.at[s])

    def flush():
        return pltpu.make_async_copy(acc.at[0], own_out, loc_sem.at[9])

    common_sent, common_events, common_count = sent[:], events[:], counter[0]

    @pl.when(heavy)
    def _():
        sent[:], events[:] = [], common_events[:]
        cps = []
        for k in range(5):
            tile1(k)
            relay((0, 0, 2, 2, 0)[k])
            if k < 3:
                contrib(0, 0, 8, 1, k)
                relay((0, 2, 2)[k])
        contrib(0, 0, 8, 1, 3)
        relay(2)
        arrive_meta(2)
        for k in range(5):
            wait_y(2, k)
        transpose_pairs(2, 0, PDEV)
        for j in range(4):
            build_bd(2, j)
        for k in range(4):
            contrib(2, 0, 8, 1, k)
            relay((2, 0, 2, 0)[k])
        for b in range(4):
            go(cps, return2(b))
        for k in range(4):
            contrib_pair(2 * k, 2, 2)
            relay((2, 0, 30, 0)[k])
        wait_slabs()
        exchange(1, 0, 4)
        go(cps, return1(0))
        go(cps, return1(1))
        exchange(1, 4, 4)
        for k in (2, 3, 4):
            go(cps, return1(k))
        exchange(0, 0, 8)
        flush().start()
        for cp in cps + sent:
            cp().wait_send()

    counter[0] = common_count

    @pl.when(jnp.logical_not(heavy))
    def _():
        sent[:], events[:] = [], common_events[:]
        cps = []
        relay(6)
        tile1(0)
        relay(4)
        tile1(1)
        relay(30)
        contrib(0, 0, 8, 1, 0)
        contrib(0, 0, 8, 1, 1)
        wait_slabs()
        exchange(1, 0, 4)
        go(cps, return1(0))
        go(cps, return1(1))
        exchange(0, 0, 4)
        tile1(2)
        exchange(1, 4, 2)
        go(cps, return1(2))
        for k in (3, 4):
            tile1(k)
            exchange(1, STEPS[k][0], 1)
            go(cps, return1(k))
        contrib(0, 0, 8, 1, 2)
        exchange(0, 4, 4)
        contrib(0, 0, 8, 1, 3)
        flush().start()
        for cp in cps + sent:
            cp().wait_send()

    sent[:] = common_sent

    flush().wait()
    for k, (lo, n) in enumerate(STEPS):
        arrival(rin1.at[pl.ds(lo, n)], r_sem.at[0, k])

    @pl.when(sender2)
    def _():
        for k in range(4):
            arrival(rin2.at[pl.ds(2 * k, 2)], r_sem.at[1, k])
        for cp in sent_pred:
            cp().wait_send()

    for cp in sent:
        cp().wait_send()


def on_device(slab, owner, orbs, bases, amps, coupled, coupled_len):
    any_ = pl.BlockSpec(memory_space=pl.ANY)
    dma = pltpu.SemaphoreType.DMA
    def shape(t):
        return jax.ShapeDtypeStruct((PDEV, NPNO, NPNO), t)

    own, back1, back2 = pl.pallas_call(
        kernel,
        out_shape=[shape(F32), shape(BF16), shape(BF16)],
        in_specs=[any_] * 7,
        out_specs=[any_] * 3,
        scratch_shapes=[
            pltpu.VMEM((3, PDEV, NORB, NPNO), BF16),
            pltpu.VMEM((3, PDEV, NPNO, NPNO), BF16),
            pltpu.VMEM((3, PDEV, 32), jnp.int32),
            pltpu.VMEM((3, PDEV, 32), jnp.int32),
            pltpu.VMEM((2, PDEV), jnp.int32),
            pltpu.VMEM((2, PDEV), jnp.int32),
            pltpu.SMEM((3, PDEV), jnp.int32),
            pltpu.SMEM((2, 2, PDEV), jnp.int32),
            pltpu.SMEM((32,), jnp.int32),
            pltpu.VMEM((32, HALF, NORB), BF16),
            pltpu.VMEM((3, PDEV, NPNO, NORB), BF16),
            pltpu.VMEM((3, 4, 2 * NPNO, 2 * NPNO), BF16),
            pltpu.VMEM((3, PDEV, NPNO, NPNO), F32),
            pltpu.VMEM((PDEV, NAUX, NPNO), BF16),
            pltpu.VMEM((2, PDEV, NPNO, NPNO), BF16),
            dma((120,)),
            dma((2, 5, 2)),
            dma((2, 3)),
            dma((2, 5)),
            dma((32,)),
            dma((32,)),
            dma((12,)),
        ],
        compiler_params=pltpu.CompilerParams(
            collective_id=0, has_side_effects=True, vmem_limit_bytes=56 * 1024 * 1024),
        name="residual",
    )(slab[0], bases, amps, coupled, coupled_len, orbs.T, owner)
    return own + back1.astype(F32) + back2.astype(F32)


def solution(mesh):
    pair = ("grp", "dev")
    in_specs = (
        P("dev", None, None), P(), P(pair, None), P(pair, None, None),
        P(pair, None, None), P(pair, None), P(pair),
    )
    return jax.shard_map(
        on_device, mesh=mesh, in_specs=in_specs, out_specs=P(pair, None, None), check_vma=False)
```
